32 devices in a mesh: clips: 2 (over x), seq: 8 (over z, y), head: 2 (over core).
Axes of the slice: x: 2, y: 2, z: 4, core: 2. Of those that a mesh axis runs over, the one named last changes fastest.
Arguments:
- video_q: bfloat16 [2048, 2048], P(('clips', 'seq'), 'head'), parts along dimension 0, may hold values from -105 to 105
- video_k: bfloat16 [2048, 2048], P(('clips', 'seq'), 'head'), parts along dimension 0, may hold values from -5 to 5
- video_v: bfloat16 [2048, 2048], P(('clips', 'seq'), 'head'), parts along dimension 0, may hold values from -6 to 6
- audio_q: bfloat16 [512, 2048], P(('clips', 'seq'), 'head'), parts along dimension 0, may hold values from -105 to 105
- audio_k: bfloat16 [512, 2048], P(('clips', 'seq'), 'head'), parts along dimension 0, may hold values from -5 to 5
- audio_v: bfloat16 [512, 2048], P(('clips', 'seq'), 'head'), parts along dimension 0, may hold values from -6 to 6
- video_query_gain: float32 [2048], P('head'), may hold values from 1 to 2
- video_key_gain: float32 [2048], P('head'), may hold values from 1 to 2
- audio_query_gain: float32 [2048], P('head'), may hold values from 1 to 2
- audio_key_gain: float32 [2048], P('head'), may hold values from 1 to 2
Outputs:
- video_mixed: bfloat16 [2048, 2048], P(('clips', 'seq'), 'head'), parts along dimension 0
- audio_mixed: bfloat16 [512, 2048], P(('clips', 'seq'), 'head'), parts along dimension 0
The draws below stay inside these ranges and needn't reach their ends.
There are 2 independent parts, one for each index of `clips`. The reference program is written for one: setup_inputs(seed, part) draws one part's arguments, and reference() takes and returns one part's arrays. A program takes and returns all parts, laid end to end along the dimension named above; an argument that names none is the same for every part. Nothing has to cross between parts.
All inputs are finite; a program needn't handle non-finite values.
Results may differ from the reference program's by a relative error of at most 0.02.
Values may be sent and summed in bfloat16 or wider, within the bound.
A program may use at most 128 MiB of HBM per device.

```python
import math
import jax
import jax.numpy as jnp
from jax import lax

HEAD_DIM = 128
VIDEO_HEADS = 16
AUDIO_HEADS = 16
VTOKENS = 1024
ATOKENS = 256


def aligned_pair(key, row_count, col_count):
    queries = jnp.clip(jax.random.normal(jax.random.fold_in(key, 31), (row_count, col_count), jnp.float32), -4.0, 4.0) * 1.25
    key_rows = jnp.clip(jax.random.normal(jax.random.fold_in(key, 37), (row_count, col_count), jnp.float32), -4.0, 4.0) * 1.25
    key_rows = key_rows.at[0, 0].set(5.0)
    key_rows = key_rows.at[1, 1].set(-5.0)
    return (queries, key_rows)


def draw_video_q(key, part):
    return aligned_pair(key, VTOKENS, VIDEO_HEADS * HEAD_DIM)[0].astype(jnp.bfloat16)


def draw_video_k(key, part):
    return aligned_pair(key, VTOKENS, VIDEO_HEADS * HEAD_DIM)[1].astype(jnp.bfloat16)


def draw_audio_q(key, part):
    return aligned_pair(key, ATOKENS, AUDIO_HEADS * HEAD_DIM)[0].astype(jnp.bfloat16)


def draw_audio_k(key, part):
    return aligned_pair(key, ATOKENS, AUDIO_HEADS * HEAD_DIM)[1].astype(jnp.bfloat16)


def steps_of(key, shape, pieces, low, high):
    loudness, own = 1.0, jax.random.fold_in(key, 6)
    for dim, parts in pieces:
        heights = jnp.exp(jax.random.uniform(jax.random.fold_in(own, dim), (parts,), jnp.float32, low / len(pieces), high / len(pieces)))
        loudness = loudness * jnp.repeat(heights, shape[dim] // parts).reshape([-1 if axis == dim else 1 for axis in range(len(shape))])
    return loudness


def bell_draw(key, extent, deviation, most, cuts=(), kind=jnp.bfloat16):
    array = jax.random.normal(key, extent, jnp.float32) * deviation
    if len(cuts) > 0:
        array = steps_of(key, extent, cuts, -0.22, 0.18) * array
    return jnp.clip(array, min=-most, max=most).astype(kind)


def setup_inputs(seed: int = 0, part: int = 0) -> dict:
    seeds = jax.random.split(jax.random.key(seed), 11)
    own_keys = jax.random.split(jax.random.fold_in(seeds[10], part), 11)
    video_q = draw_video_q(jax.random.fold_in(jax.random.fold_in(seeds[10], part), 71), part)
    video_k = draw_video_k(jax.random.fold_in(jax.random.fold_in(seeds[10], part), 71), part)
    video_v = bell_draw(own_keys[2], (VTOKENS, VIDEO_HEADS * HEAD_DIM), 1.0, 6.0, ((0, 8), (1, 2)))
    audio_q = draw_audio_q(jax.random.fold_in(jax.random.fold_in(seeds[10], part), 71), part)
    audio_k = draw_audio_k(jax.random.fold_in(jax.random.fold_in(seeds[10], part), 71), part)
    audio_v = bell_draw(own_keys[5], (ATOKENS, AUDIO_HEADS * HEAD_DIM), 1.0, 6.0, ((0, 8), (1, 2)))
    video_query_gain = jnp.clip(jnp.exp(math.log(2.0) - 0.6931472 * jax.random.uniform(seeds[6], (VIDEO_HEADS * HEAD_DIM,), jnp.float32) ** steps_of(seeds[6], (VIDEO_HEADS * HEAD_DIM,), ((0, 2),), -0.2, 0.2)), 1.0, 2.0)
    video_key_gain = jnp.clip(jnp.exp(math.log(2.0) - 0.6931472 * jax.random.uniform(seeds[7], (VIDEO_HEADS * HEAD_DIM,), jnp.float32) ** steps_of(seeds[7], (VIDEO_HEADS * HEAD_DIM,), ((0, 2),), -0.2, 0.2)), 1.0, 2.0)
    audio_query_gain = jnp.clip(jnp.exp(math.log(2.0) - 0.6931472 * jax.random.uniform(seeds[8], (AUDIO_HEADS * HEAD_DIM,), jnp.float32) ** steps_of(seeds[8], (AUDIO_HEADS * HEAD_DIM,), ((0, 2),), -0.2, 0.2)), 1.0, 2.0)
    audio_key_gain = jnp.clip(jnp.exp(math.log(2.0) - 0.6931472 * jax.random.uniform(seeds[9], (AUDIO_HEADS * HEAD_DIM,), jnp.float32) ** steps_of(seeds[9], (AUDIO_HEADS * HEAD_DIM,), ((0, 2),), -0.2, 0.2)), 1.0, 2.0)
    return dict(video_q=video_q, video_k=video_k, video_v=video_v, audio_q=audio_q, audio_k=audio_k, audio_v=audio_v, video_query_gain=video_query_gain, video_key_gain=video_key_gain, audio_query_gain=audio_query_gain, audio_key_gain=audio_key_gain)


def softmax_attend(queries, key_rows, values, head_count):
    query_count = queries.shape[0]

    def per_head(index):
        offset = (index * HEAD_DIM).astype(jnp.int32)
        left = lax.dynamic_slice_in_dim(queries, offset, HEAD_DIM, 1)
        right = lax.dynamic_slice_in_dim(key_rows, offset, HEAD_DIM, 1)
        value_cols = lax.dynamic_slice_in_dim(values, offset, HEAD_DIM, 1)
        scores = jnp.dot(left, right.T, preferred_element_type=jnp.float32) * HEAD_DIM ** (-0.5)
        weights = jnp.exp(scores - lax.optimization_barrier(jnp.max(scores, axis=1, keepdims=True)))
        row_total = lax.optimization_barrier(jnp.sum(weights, axis=1))
        output = jnp.dot(weights.astype(jnp.bfloat16), value_cols, preferred_element_type=jnp.float32)
        return output / row_total[:, None]
    stacked = lax.map(per_head, jnp.arange(head_count, dtype=jnp.int32))
    return jnp.transpose(stacked, (1, 0, 2)).reshape(query_count, head_count * HEAD_DIM)

def normed(tokens, gain_row):
    count = tokens.shape[0]
    head_count = tokens.shape[1] // HEAD_DIM
    entries = tokens.astype(jnp.float32).reshape(count, head_count, HEAD_DIM)
    scaled = entries * lax.rsqrt(lax.optimization_barrier(jnp.mean(entries * entries, axis=2, keepdims=True)) + 1e-06)
    return (scaled.reshape(count, head_count * HEAD_DIM) * gain_row).astype(jnp.bfloat16)

def reference(video_q, video_k, video_v, audio_q, audio_k, audio_v, video_query_gain, video_key_gain, audio_query_gain, audio_key_gain):
    video_self = softmax_attend(video_q, video_k, video_v, VIDEO_HEADS).astype(jnp.bfloat16)
    audio_self = softmax_attend(audio_q, audio_k, audio_v, AUDIO_HEADS).astype(jnp.bfloat16)
    video_cross = softmax_attend(normed(video_self, video_query_gain), normed(audio_self, audio_key_gain), audio_self, VIDEO_HEADS)
    audio_cross = softmax_attend(normed(audio_self, audio_query_gain), normed(video_self, video_key_gain), video_self, AUDIO_HEADS)
    video_mixed = (video_self.astype(jnp.float32) + video_cross).astype(jnp.bfloat16)
    audio_mixed = (audio_self.astype(jnp.float32) + audio_cross).astype(jnp.bfloat16)
    return (video_mixed, audio_mixed)
```

```python
import functools
import math

import jax
import jax.numpy as jnp
from jax import lax
from jax.experimental import pallas as pl
from jax.experimental.pallas import tpu as pltpu
from jax.sharding import PartitionSpec as P

HEAD_DIM = 128
EXP2_SCALE = HEAD_DIM ** (-0.5) * math.log2(math.e)


def normed(tokens, gain_row):
    count = tokens.shape[0]
    head_count = tokens.shape[1] // HEAD_DIM
    entries = tokens.astype(jnp.float32).reshape(count, head_count, HEAD_DIM)
    scaled = entries * lax.rsqrt(jnp.mean(entries * entries, axis=2, keepdims=True) + 1e-06)
    return (scaled.reshape(count, head_count * HEAD_DIM) * gain_row).astype(jnp.bfloat16)


def start_state(row_count, head_count):
    return (
        jnp.full((head_count, row_count), -1e30, jnp.float32),
        jnp.zeros((head_count, row_count), jnp.float32),
        jnp.zeros((row_count, head_count, HEAD_DIM), jnp.float32),
    )


def folding(queries, prepare):
    head_count = queries.shape[1]

    def fold_step(state_now, pieces, offset):
        key_rows, values = prepare(pieces)
        key_rows = key_rows.reshape(key_rows.shape[0], head_count, HEAD_DIM)
        values = values.reshape(values.shape[0], head_count, HEAD_DIM)
        scores = jnp.einsum(
            "qhd,khd->hqk", queries, key_rows, preferred_element_type=jnp.float32
        ) * HEAD_DIM ** (-0.5)
        running_max, row_total, accumulated = state_now
        new_max = jnp.maximum(running_max, jnp.max(scores, axis=2))
        rescale = jnp.exp(running_max - new_max)
        weights = jnp.exp(scores - new_max[:, :, None])
        row_total = jnp.sum(weights, axis=2)
        update = jnp.einsum(
            "hqk,khd->qhd", weights.astype(jnp.bfloat16), values, preferred_element_type=jnp.float32
        )
        accumulated = accumulated * rescale.T[:, :, None] + update
        return (new_max, row_total, accumulated)

    return fold_step


def finish(state_now):
    running_max, row_total, accumulated = state_now
    result = accumulated / row_total.T[:, :, None]
    return result.reshape(result.shape[0], result.shape[1] * HEAD_DIM)


def as_heads(tokens):
    return tokens.reshape(tokens.shape[0], tokens.shape[1] // HEAD_DIM, HEAD_DIM)


def keep_pair(pieces):
    return pieces


def per_device(
    video_q,
    video_k,
    video_v,
    audio_q,
    audio_k,
    audio_v,
    video_query_gain,
    video_key_gain,
    audio_query_gain,
    audio_key_gain,
):
    head_count = video_q.shape[1] // HEAD_DIM
    video_rows = video_q.shape[0]
    audio_rows = audio_q.shape[0]
    video_state = folding(as_heads(video_q), keep_pair)(
        start_state(video_rows, head_count),
        (
            lax.all_gather(video_k, "seq", axis=0, tiled=True),
            lax.all_gather(video_v, "seq", axis=0, tiled=True),
        ),
        jnp.int32(0),
    )
    video_self = finish(video_state).astype(jnp.bfloat16)
    audio_state = folding(as_heads(audio_q), keep_pair)(
        start_state(audio_rows, head_count),
        (
            lax.all_gather(audio_k, "seq", axis=0, tiled=True),
            lax.all_gather(audio_v, "seq", axis=0, tiled=True),
        ),
        jnp.int32(0),
    )
    audio_self = finish(audio_state).astype(jnp.bfloat16)
    audio_whole = lax.all_gather(audio_self, "seq", axis=0, tiled=True)
    video_queries = as_heads(normed(video_self, video_query_gain))
    cross_step = folding(video_queries, keep_pair)
    video_cross = finish(
        cross_step(
            start_state(video_rows, head_count),
            (normed(audio_whole, audio_key_gain), audio_whole),
            0,
        )
    )
    audio_queries = normed(audio_self, audio_query_gain)

    def prepare_video(shard_rows):
        return (normed(shard_rows, video_key_gain), shard_rows)

    audio_state_cross = folding(as_heads(audio_queries), prepare_video)(
        start_state(audio_rows, head_count),
        lax.all_gather(video_self, "seq", axis=0, tiled=True),
        jnp.int32(0),
    )
    audio_cross = finish(audio_state_cross)
    video_mixed = (video_self.astype(jnp.float32) + video_cross).astype(jnp.bfloat16)
    audio_mixed = (audio_self.astype(jnp.float32) + audio_cross).astype(jnp.bfloat16)
    return (video_mixed, audio_mixed)


def attend_kernel(
    n,
    video_q,
    video_k,
    video_v,
    audio_q,
    audio_k,
    audio_v,
    video_query_gain_in,
    video_key_gain_in,
    audio_query_gain_in,
    audio_key_gain_in,
    video_out,
    audio_out,
    vq,
    vk,
    vv,
    aq,
    ak,
    av,
    audio_self,
    audio_queries,
    audio_keys,
    audio_sum,
    video_mixed,
    audio_mixed,
    send_sem,
    recv_sem,
    own_sem,
    out_send_sem,
    out_recv_sem,
    out_own_sem,
    in_sem,
    video_query_gain,
    video_key_gain,
    audio_query_gain,
    audio_key_gain,
    gain_sem,
):
    me = lax.axis_index("seq")
    rows = video_q.shape[0]
    arows = audio_q.shape[0]

    width = n // 4
    place, lane = me // width, lax.rem(me, width)
    middle = jnp.logical_or(place == 1, place == 2)
    edge = jnp.logical_not(middle)
    inner = lax.select(place < 2, 1, 2)
    outer = lax.select(place < 2, 0, 3)

    def device(column, step):
        return column * width + lax.rem(lane + step, width)

    mates = [device(place, step) for step in range(1, width)]
    beside = [device(inner + outer - place, step) for step in range(width)]
    far_middle = [device(3 - inner, step) for step in range(width)]
    far_edge = [device(3 - outer, step) for step in range(width)]

    def head_columns(index):
        return pl.ds(pl.multiple_of(index * HEAD_DIM, HEAD_DIM), HEAD_DIM)

    def token_rows(index, count):
        return pl.ds(pl.multiple_of(index * count, count), count)

    ins = (
        (audio_k, ak, arows),
        (audio_v, av, arows),
        (audio_q, aq, arows),
        (video_k, vk, rows),
        (video_v, vv, rows),
        (video_q, vq, rows),
    )

    def own_in(kind):
        source, target, count = ins[kind]
        return pltpu.make_async_copy(
            source.at[:, head_columns(me)],
            target.at[token_rows(me, count), pl.ds(0, HEAD_DIM)],
            own_sem.at[kind],
        )

    def sent_in(kind, peer):
        source, target, count = ins[kind]
        return pltpu.make_async_remote_copy(
            src_ref=source.at[:, head_columns(peer)],
            dst_ref=target.at[token_rows(me, count), pl.ds(0, HEAD_DIM)],
            send_sem=send_sem.at[kind, peer],
            recv_sem=recv_sem.at[kind, me],
            device_id={"seq": peer},
            device_id_type=pl.DeviceIdType.MESH,
        )

    def received_in(kind, peer):
        source, target, count = ins[kind]
        return pltpu.make_async_remote_copy(
            src_ref=source.at[:, head_columns(peer)],
            dst_ref=target.at[token_rows(peer, count), pl.ds(0, HEAD_DIM)],
            send_sem=send_sem.at[kind, peer],
            recv_sem=recv_sem.at[kind, peer],
            device_id={"seq": peer},
            device_id_type=pl.DeviceIdType.MESH,
        )

    outs = ((audio_mixed, audio_out, arows), (video_mixed, video_out, rows))

    def own_out(kind):
        source, target, count = outs[kind]
        return pltpu.make_async_copy(
            source.at[token_rows(me, count), :],
            target.at[:, head_columns(me)],
            out_own_sem.at[kind],
        )

    def sent_out(kind, peer):
        source, target, count = outs[kind]
        return pltpu.make_async_remote_copy(
            src_ref=source.at[token_rows(peer, count), :],
            dst_ref=target.at[:, head_columns(me)],
            send_sem=out_send_sem.at[kind, peer],
            recv_sem=out_recv_sem.at[kind, me],
            device_id={"seq": peer},
            device_id_type=pl.DeviceIdType.MESH,
        )

    def received_out(kind, peer):
        source, target, count = outs[kind]
        return pltpu.make_async_remote_copy(
            src_ref=source.at[token_rows(peer, count), :],
            dst_ref=target.at[:, head_columns(peer)],
            send_sem=out_send_sem.at[kind, peer],
            recv_sem=out_recv_sem.at[kind, peer],
            device_id={"seq": peer},
            device_id_type=pl.DeviceIdType.MESH,
        )

    def signal(semaphore, peer):
        pl.semaphore_signal(
            semaphore,
            inc=1,
            device_id={"seq": peer},
            device_id_type=pl.DeviceIdType.MESH,
        )

    def send(kinds, peers):
        for kind in kinds:
            for peer in peers:
                sent_in(kind, peer).start()

    barrier = pltpu.get_barrier_semaphore()
    first_lane = lane == 0
    core = lax.axis_index("head")
    leader = core == 0

    def signal_core(semaphore):
        pl.semaphore_signal(
            semaphore,
            inc=1,
            device_id={"head": 1 - core},
            device_id_type=pl.DeviceIdType.MESH,
        )

    def follow():
        @pl.when(leader)
        def _():
            signal_core(in_sem.at[6])

        @pl.when(jnp.logical_not(leader))
        def _():
            pl.semaphore_wait(in_sem.at[6], 1)

    early, keys, queries_in = (0, 1, 2), (3, 4), (5,)

    @pl.when(middle)
    def _():
        signal(barrier, far_middle[0])
        signal(barrier, beside[0])

        @pl.when(jnp.logical_not(leader))
        def _():
            signal_core(barrier)

        pl.semaphore_wait(barrier, lax.select(first_lane, 1, 2) + lax.select(leader, 1, 0))

        @pl.when(first_lane)
        def _():
            for peer in mates:
                signal(barrier, peer)

        send(early, far_middle[:1])
        send(keys, far_middle[:1])

        @pl.when(first_lane)
        def _():
            pl.semaphore_wait(in_sem.at[0], len(mates))

        @pl.when(jnp.logical_not(first_lane))
        def _():
            signal(in_sem.at[0], me - lane)

        send(early, far_middle[1:])
        pl.semaphore_wait(in_sem.at[1], 1)
        signal(in_sem.at[2], far_middle[0])
        signal(in_sem.at[5], beside[0])
        send(early, beside[:1] + mates)
        pl.semaphore_wait(in_sem.at[2], 1)
        for peer in mates:
            signal(in_sem.at[3], peer)
        send(early, far_edge[:1])
        send(keys, far_edge[:1])
        send(keys, beside[:1] + mates)
        pl.semaphore_wait(in_sem.at[3], len(mates))
        follow()
        signal(in_sem.at[4], beside[0])
        send(early, far_edge[1:] + beside[1:])
        send(keys, far_edge[1:] + beside[1:])
        send(keys, far_middle[1:])
        send(queries_in, beside + mates)
        send(queries_in, far_edge + far_middle)

    @pl.when(edge)
    def _():
        @pl.when(jnp.logical_not(leader))
        def _():
            signal_core(barrier)

        pl.semaphore_wait(barrier, lax.select(leader, 2, 1))
        signal(in_sem.at[1], beside[0])
        pl.semaphore_wait(in_sem.at[5], 1)
        send(early, far_middle[:1] + beside[:1])
        send(keys, far_middle[:1] + beside[:1])
        pl.semaphore_wait(in_sem.at[4], 1)
        follow()

        send(early, far_edge + far_middle[1:])
        send(keys, far_edge + far_middle[1:])
        send(early, mates + beside[1:])
        send(keys, mates + beside[1:])
        send(queries_in, mates + beside)

    gains = [
        pltpu.make_async_copy(source, target, gain_sem.at[index])
        for index, (source, target) in enumerate(
            (
                (video_query_gain_in, video_query_gain),
                (video_key_gain_in, video_key_gain),
                (audio_query_gain_in, audio_query_gain),
                (audio_key_gain_in, audio_key_gain),
            )
        )
    ]
    for gain in gains:
        gain.start()
    for kind in range(len(ins)):
        own_in(kind).start()

    ones = jnp.ones((arows * n, HEAD_DIM), jnp.bfloat16)
    av[:, HEAD_DIM:] = ones
    audio_self[:, HEAD_DIM:] = ones
    ones = jnp.ones((rows * n, HEAD_DIM), jnp.bfloat16)
    vv[:, HEAD_DIM:] = ones
    audio_sum[...] = jnp.zeros_like(audio_sum)

    others = mates + beside + far_middle + far_edge

    def wait_kinds(kinds):
        for kind in kinds:
            own_in(kind).wait()

        for peer in others:
            for kind in kinds:
                received_in(kind, peer).wait_recv()

    def dot_t(left, right):
        return lax.dot_general(
            left, right, (((1,), (1,)), ((), ())), preferred_element_type=jnp.float32
        )

    def dot(left, right):
        return jnp.dot(left, right, preferred_element_type=jnp.float32)

    def self_attend(queries, key_rows, values):
        scores = dot_t(queries, key_rows)
        largest = jnp.max(scores, axis=1, keepdims=True)
        weights = jnp.exp2((scores - largest) * EXP2_SCALE).astype(jnp.bfloat16)
        both = dot(weights, values)
        return (both[:, :HEAD_DIM] / both[:, HEAD_DIM:]).astype(jnp.bfloat16)

    def unit(tokens):
        entries = tokens.astype(jnp.float32)
        mean = jnp.mean(entries * entries, axis=1, keepdims=True)
        return entries * lax.rsqrt(mean + 1e-06)

    own_head = pl.ds(me, 1)
    for gain in gains:
        gain.wait()
    wait_kinds((0, 1, 2))
    tokens = self_attend(aq[...], ak[...], av[...])
    audio_self[:, :HEAD_DIM] = tokens
    scaled = unit(tokens)
    audio_queries[...] = (scaled * audio_query_gain[own_head, :]).astype(jnp.bfloat16)
    audio_keys[...] = (scaled * audio_key_gain[own_head, :]).astype(jnp.bfloat16)

    wait_kinds((3, 4))

    @pl.when(edge)
    def _():
        send(queries_in, far_edge + far_middle)


    def self_part(peers):
        here = [token_rows(peer, rows) for peer in peers]
        tokens = self_attend(jnp.concatenate([vq[one, :] for one in here], 0), vk[...], vv[...])
        scaled = unit(tokens)
        queries = (scaled * video_query_gain[own_head, :]).astype(jnp.bfloat16)
        key_rows = (scaled * video_key_gain[own_head, :]).astype(jnp.bfloat16)
        return tokens, queries, key_rows

    def audio_part(tokens, key_rows):
        weights = jnp.exp2(dot_t(audio_queries[...], key_rows) * EXP2_SCALE)
        values = jnp.concatenate([tokens, jnp.ones_like(tokens)], 1)
        audio_sum[...] += dot(weights.astype(jnp.bfloat16), values)

    def video_part(peers, tokens, queries):
        weights = jnp.exp2(dot_t(queries, audio_keys[...]) * EXP2_SCALE)
        both = dot(weights.astype(jnp.bfloat16), audio_self[...])
        cross = both[:, :HEAD_DIM] / both[:, HEAD_DIM:]
        mixed = (tokens.astype(jnp.float32) + cross).astype(jnp.bfloat16)
        for index, peer in enumerate(peers):
            video_mixed[token_rows(peer, rows), :] = mixed[index * rows : (index + 1) * rows]

    order = [me] + others
    plan = ((0, 1), (2, 3), (6, 7), (4, 5))
    for turn, members in enumerate(plan):
        last = turn + 1 == len(plan)
        peers = [order[index] for index in members]
        for index, peer in zip(members, peers):
            if index == 0:
                own_in(5).wait()
            else:
                received_in(5, peer).wait_recv()
        tokens, queries, key_rows = self_part(peers)
        if last:
            audio_part(tokens, key_rows)
            both = audio_sum[...]
            cross = both[:, :HEAD_DIM] / both[:, HEAD_DIM:]
            audio_mixed[...] = (
                audio_self[:, :HEAD_DIM].astype(jnp.float32) + cross
            ).astype(jnp.bfloat16)
            own_out(0).start()
            for peer in reversed(others):
                sent_out(0, peer).start()
        video_part(peers, tokens, queries)
        for index, peer in zip(members, peers):
            if index == 0:
                own_out(1).start()
            else:
                sent_out(1, peer).start()
        if not last:
            audio_part(tokens, key_rows)

    own_out(0).wait()
    own_out(1).wait()
    for peer in others:
        for kind in range(len(ins)):
            sent_in(kind, peer).wait_send()
        for kind in range(len(outs)):
            sent_out(kind, peer).wait_send()
    for peer in others:
        for kind in range(len(outs)):
            received_out(kind, peer).wait_recv()


def pass_on_kernel(video_in, audio_in, video_out, audio_out, sem):
    copies = (
        pltpu.make_async_copy(video_in, video_out, sem.at[0]),
        pltpu.make_async_copy(audio_in, audio_out, sem.at[1]),
    )
    for copy in copies:
        copy.start()
    for copy in copies:
        copy.wait()


GROUP = 2
KERNEL_BYTES = 24 * 2**20


def head_per_device(n, *arrays):
    video_q, audio_q = arrays[0], arrays[3]
    tokens, atokens = video_q.shape[0] * n, audio_q.shape[0] * n
    bf16, f32 = jnp.bfloat16, jnp.float32
    gains = [gain.reshape(n, HEAD_DIM) for gain in arrays[6:]]
    anywhere = pl.BlockSpec(memory_space=pl.ANY)
    operands = [
        pltpu.with_memory_space_constraint(one, pltpu.HBM) for one in (*arrays[:6], *gains)
    ]
    results = pl.pallas_call(
        functools.partial(attend_kernel, n),
        out_shape=(
            jax.ShapeDtypeStruct(video_q.shape, bf16),
            jax.ShapeDtypeStruct(audio_q.shape, bf16),
        ),
        in_specs=[anywhere] * 10,
        out_specs=(anywhere, anywhere),
        scratch_shapes=[
            pltpu.VMEM((tokens, HEAD_DIM), bf16),
            pltpu.VMEM((tokens, HEAD_DIM), bf16),
            pltpu.VMEM((tokens, 2 * HEAD_DIM), bf16),
            pltpu.VMEM((atokens, HEAD_DIM), bf16),
            pltpu.VMEM((atokens, HEAD_DIM), bf16),
            pltpu.VMEM((atokens, 2 * HEAD_DIM), bf16),
            pltpu.VMEM((atokens, 2 * HEAD_DIM), bf16),
            pltpu.VMEM((atokens, HEAD_DIM), bf16),
            pltpu.VMEM((atokens, HEAD_DIM), bf16),
            pltpu.VMEM((atokens, 2 * HEAD_DIM), f32),
            pltpu.VMEM((tokens, HEAD_DIM), bf16),
            pltpu.VMEM((atokens, HEAD_DIM), bf16),
            pltpu.SemaphoreType.DMA((6, n)),
            pltpu.SemaphoreType.DMA((6, n)),
            pltpu.SemaphoreType.DMA((6,)),
            pltpu.SemaphoreType.DMA((2, n)),
            pltpu.SemaphoreType.DMA((2, n)),
            pltpu.SemaphoreType.DMA((2,)),
            pltpu.SemaphoreType.REGULAR((7,)),
            *[pltpu.VMEM((n, HEAD_DIM), f32)] * 4,
            pltpu.SemaphoreType.DMA((4,)),
        ],
        compiler_params=pltpu.CompilerParams(
            collective_id=0, has_side_effects=True, vmem_limit_bytes=KERNEL_BYTES
        ),
    )(*operands)
    return pl.pallas_call(
        pass_on_kernel,
        out_shape=(
            jax.ShapeDtypeStruct(video_q.shape, bf16),
            jax.ShapeDtypeStruct(audio_q.shape, bf16),
        ),
        in_specs=[anywhere] * 2,
        out_specs=(anywhere, anywhere),
        scratch_shapes=[pltpu.SemaphoreType.DMA((2,))],
        compiler_params=pltpu.CompilerParams(vmem_limit_bytes=KERNEL_BYTES // 4),
    )(*results)


def solution(mesh):
    in_specs = (
        P(("clips", "seq"), "head"),
        P(("clips", "seq"), "head"),
        P(("clips", "seq"), "head"),
        P(("clips", "seq"), "head"),
        P(("clips", "seq"), "head"),
        P(("clips", "seq"), "head"),
        P("head"),
        P("head"),
        P("head"),
        P("head"),
    )
    out_specs = (P(("clips", "seq"), "head"), P(("clips", "seq"), "head"))
    sizes = dict(mesh.shape)

    def body(*arrays):
        video_q, audio_q = arrays[0], arrays[3]
        if (
            video_q.shape[1] == sizes["seq"] * HEAD_DIM
            and sizes["seq"] == 8
            and video_q.shape[0] % 16 == 0
            and audio_q.shape[0] % 16 == 0
        ):
            return head_per_device(sizes["seq"], *arrays)
        return per_device(*arrays)

    return jax.shard_map(
        body, mesh=mesh, in_specs=in_specs, out_specs=out_specs, check_vma=False
    )
```

```python
import functools
import math

import jax
import jax.numpy as jnp
from jax import lax
from jax.experimental import pallas as pl
from jax.experimental.pallas import tpu as pltpu
from jax.sharding import PartitionSpec as P

HEAD_DIM = 128
EXP2_SCALE = HEAD_DIM ** (-0.5) * math.log2(math.e)


def normed(tokens, gain_row):
    count = tokens.shape[0]
    head_count = tokens.shape[1] // HEAD_DIM
    entries = tokens.astype(jnp.float32).reshape(count, head_count, HEAD_DIM)
    scaled = entries * lax.rsqrt(jnp.mean(entries * entries, axis=2, keepdims=True) + 1e-06)
    return (scaled.reshape(count, head_count * HEAD_DIM) * gain_row).astype(jnp.bfloat16)


def start_state(row_count, head_count):
    return (
        jnp.full((head_count, row_count), -1e30, jnp.float32),
        jnp.zeros((head_count, row_count), jnp.float32),
        jnp.zeros((row_count, head_count, HEAD_DIM), jnp.float32),
    )


def folding(queries, prepare):
    head_count = queries.shape[1]

    def fold_step(state_now, pieces, offset):
        key_rows, values = prepare(pieces)
        key_rows = key_rows.reshape(key_rows.shape[0], head_count, HEAD_DIM)
        values = values.reshape(values.shape[0], head_count, HEAD_DIM)
        scores = jnp.einsum(
            "qhd,khd->hqk", queries, key_rows, preferred_element_type=jnp.float32
        ) * HEAD_DIM ** (-0.5)
        running_max, row_total, accumulated = state_now
        new_max = jnp.maximum(running_max, jnp.max(scores, axis=2))
        rescale = jnp.exp(running_max - new_max)
        weights = jnp.exp(scores - new_max[:, :, None])
        row_total = jnp.sum(weights, axis=2)
        update = jnp.einsum(
            "hqk,khd->qhd", weights.astype(jnp.bfloat16), values, preferred_element_type=jnp.float32
        )
        accumulated = accumulated * rescale.T[:, :, None] + update
        return (new_max, row_total, accumulated)

    return fold_step


def finish(state_now):
    running_max, row_total, accumulated = state_now
    result = accumulated / row_total.T[:, :, None]
    return result.reshape(result.shape[0], result.shape[1] * HEAD_DIM)


def as_heads(tokens):
    return tokens.reshape(tokens.shape[0], tokens.shape[1] // HEAD_DIM, HEAD_DIM)


def keep_pair(pieces):
    return pieces


def per_device(
    video_q,
    video_k,
    video_v,
    audio_q,
    audio_k,
    audio_v,
    video_query_gain,
    video_key_gain,
    audio_query_gain,
    audio_key_gain,
):
    head_count = video_q.shape[1] // HEAD_DIM
    video_rows = video_q.shape[0]
    audio_rows = audio_q.shape[0]
    video_state = folding(as_heads(video_q), keep_pair)(
        start_state(video_rows, head_count),
        (
            lax.all_gather(video_k, "seq", axis=0, tiled=True),
            lax.all_gather(video_v, "seq", axis=0, tiled=True),
        ),
        jnp.int32(0),
    )
    video_self = finish(video_state).astype(jnp.bfloat16)
    audio_state = folding(as_heads(audio_q), keep_pair)(
        start_state(audio_rows, head_count),
        (
            lax.all_gather(audio_k, "seq", axis=0, tiled=True),
            lax.all_gather(audio_v, "seq", axis=0, tiled=True),
        ),
        jnp.int32(0),
    )
    audio_self = finish(audio_state).astype(jnp.bfloat16)
    audio_whole = lax.all_gather(audio_self, "seq", axis=0, tiled=True)
    video_queries = as_heads(normed(video_self, video_query_gain))
    cross_step = folding(video_queries, keep_pair)
    video_cross = finish(
        cross_step(
            start_state(video_rows, head_count),
            (normed(audio_whole, audio_key_gain), audio_whole),
            0,
        )
    )
    audio_queries = normed(audio_self, audio_query_gain)

    def prepare_video(shard_rows):
        return (normed(shard_rows, video_key_gain), shard_rows)

    audio_state_cross = folding(as_heads(audio_queries), prepare_video)(
        start_state(audio_rows, head_count),
        lax.all_gather(video_self, "seq", axis=0, tiled=True),
        jnp.int32(0),
    )
    audio_cross = finish(audio_state_cross)
    video_mixed = (video_self.astype(jnp.float32) + video_cross).astype(jnp.bfloat16)
    audio_mixed = (audio_self.astype(jnp.float32) + audio_cross).astype(jnp.bfloat16)
    return (video_mixed, audio_mixed)


def attend_kernel(
    n,
    video_q,
    video_k,
    video_v,
    audio_q,
    audio_k,
    audio_v,
    video_query_gain_in,
    video_key_gain_in,
    audio_query_gain_in,
    audio_key_gain_in,
    video_out,
    audio_out,
    vq,
    vk,
    vv,
    aq,
    ak,
    av,
    audio_self,
    audio_queries,
    audio_keys,
    audio_sum,
    video_mixed,
    audio_mixed,
    send_sem,
    recv_sem,
    query_sem,
    out_send_sem,
    out_recv_sem,
    in_sem,
    all_gains,
    gain_sem,
):
    me = lax.axis_index("seq")
    rows = video_q.shape[0]
    arows = audio_q.shape[0]

    width = n // 4
    place, lane = me // width, lax.rem(me, width)
    middle = jnp.logical_or(place == 1, place == 2)
    edge = jnp.logical_not(middle)
    inner = lax.select(place < 2, 1, 2)
    outer = lax.select(place < 2, 0, 3)

    def device(column, step):
        return column * width + lax.rem(lane + step, width)

    mates = [device(place, step) for step in range(1, width)]
    beside = [device(inner + outer - place, step) for step in range(width)]
    far_middle = [device(3 - inner, step) for step in range(width)]
    far_edge = [device(3 - outer, step) for step in range(width)]

    def head_columns(index):
        return pl.ds(pl.multiple_of(index * HEAD_DIM, HEAD_DIM), HEAD_DIM)

    def token_rows(index, count):
        return pl.ds(pl.multiple_of(index * count, count), count)

    ins = (
        (audio_k, ak, arows),
        (audio_v, av, arows),
        (audio_q, aq, arows),
        (video_k, vk, rows),
        (video_v, vv, rows),
        (video_q, vq, rows),
    )

    own_class, beside_class = 0, 1
    far_class = lax.select(middle, 2, 3)
    classes = ([me] + mates, beside, far_middle, far_edge)

    def landing(kind, turn):
        return query_sem.at[turn] if kind == 5 else recv_sem.at[kind]

    def own_in(kind):
        source, target, count = ins[kind]
        return pltpu.make_async_copy(
            source.at[:, head_columns(me)],
            target.at[token_rows(me, count), pl.ds(0, HEAD_DIM)],
            landing(kind, own_class),
        )

    def sent_in(kind, peer, turn):
        source, target, count = ins[kind]
        return pltpu.make_async_remote_copy(
            src_ref=source.at[:, head_columns(peer)],
            dst_ref=target.at[token_rows(me, count), pl.ds(0, HEAD_DIM)],
            send_sem=send_sem.at[kind],
            recv_sem=landing(kind, turn),
            device_id={"seq": peer},
            device_id_type=pl.DeviceIdType.MESH,
        )

    def wait_bytes(ref, semaphore):
        pltpu.make_async_copy(ref, ref, semaphore).wait()

    def wait_in(kind):
        wait_bytes(ins[kind][1].at[:, pl.ds(0, HEAD_DIM)], recv_sem.at[kind])

    def wait_queries(turn):
        wait_bytes(vq.at[pl.ds(0, width * rows), :], query_sem.at[turn])

    def wait_sent_in(kind):
        source, target, count = ins[kind]
        sent = target.at[pl.ds(0, (n - 1) * count), pl.ds(0, HEAD_DIM)]
        wait_bytes(sent, send_sem.at[kind])

    outs = ((audio_mixed, audio_out, arows), (video_mixed, video_out, rows))

    def own_out(kind):
        source, target, count = outs[kind]
        return pltpu.make_async_copy(
            source.at[token_rows(me, count), :],
            target.at[:, head_columns(me)],
            out_recv_sem.at[kind],
        )

    def sent_out(kind, peer):
        source, target, count = outs[kind]
        return pltpu.make_async_remote_copy(
            src_ref=source.at[token_rows(peer, count), :],
            dst_ref=target.at[:, head_columns(me)],
            send_sem=out_send_sem.at[kind],
            recv_sem=out_recv_sem.at[kind],
            device_id={"seq": peer},
            device_id_type=pl.DeviceIdType.MESH,
        )

    def wait_out(kind):
        source, target, count = outs[kind]
        wait_bytes(source.at[pl.ds(0, (n - 1) * count), :], out_send_sem.at[kind])
        wait_bytes(target, out_recv_sem.at[kind])

    def signal(semaphore, peer):
        pl.semaphore_signal(
            semaphore,
            inc=1,
            device_id={"seq": peer},
            device_id_type=pl.DeviceIdType.MESH,
        )

    def send(kinds, peers):
        for kind in kinds:
            for peer in peers:
                sent_in(kind, peer, None).start()

    def send_queries(peers, turn):
        for peer in peers:
            sent_in(5, peer, turn).start()

    barrier = pltpu.get_barrier_semaphore()
    first_lane = lane == 0
    core = lax.axis_index("head")
    leader = core == 0

    def signal_core(semaphore):
        pl.semaphore_signal(
            semaphore,
            inc=1,
            device_id={"head": 1 - core},
            device_id_type=pl.DeviceIdType.MESH,
        )

    def follow():
        @pl.when(leader)
        def _():
            signal_core(in_sem.at[6])

        @pl.when(jnp.logical_not(leader))
        def _():
            pl.semaphore_wait(in_sem.at[6], 1)

    early, keys = (0, 1, 2), (3, 4)

    @pl.when(middle)
    def _():
        signal(barrier, far_middle[0])
        signal(barrier, beside[0])

        @pl.when(jnp.logical_not(leader))
        def _():
            signal_core(barrier)

        pl.semaphore_wait(barrier, lax.select(first_lane, 1, 2) + lax.select(leader, 1, 0))

        @pl.when(first_lane)
        def _():
            for peer in mates:
                signal(barrier, peer)

        send(early, far_middle[:1])
        send(keys, far_middle[:1])

        @pl.when(first_lane)
        def _():
            pl.semaphore_wait(in_sem.at[0], len(mates))

        @pl.when(jnp.logical_not(first_lane))
        def _():
            signal(in_sem.at[0], me - lane)

        send(early, far_middle[1:])
        pl.semaphore_wait(in_sem.at[1], 1)
        signal(in_sem.at[2], far_middle[0])
        signal(in_sem.at[5], beside[0])
        send(early, beside[:1] + mates)
        pl.semaphore_wait(in_sem.at[2], 1)
        for peer in mates:
            signal(in_sem.at[3], peer)
        send(early, far_edge[:1])
        send(keys, far_edge[:1])
        send(keys, beside[:1] + mates)
        pl.semaphore_wait(in_sem.at[3], len(mates))
        follow()
        signal(in_sem.at[4], beside[0])
        send(early, far_edge[1:] + beside[1:])
        send(keys, far_edge[1:] + beside[1:])
        send(keys, far_middle[1:])
        send_queries(beside, beside_class)
        send_queries(mates, own_class)
        send_queries(far_edge + far_middle, far_class)

    @pl.when(edge)
    def _():
        @pl.when(jnp.logical_not(leader))
        def _():
            signal_core(barrier)

        pl.semaphore_wait(barrier, lax.select(leader, 2, 1))
        signal(in_sem.at[1], beside[0])
        pl.semaphore_wait(in_sem.at[5], 1)
        send(early, far_middle[:1] + beside[:1])
        send(keys, far_middle[:1] + beside[:1])
        pl.semaphore_wait(in_sem.at[4], 1)
        follow()

        send(early, far_edge + far_middle[1:])
        send(keys, far_edge + far_middle[1:])
        send(early, mates + beside[1:])
        send(keys, mates + beside[1:])
        send_queries(mates, own_class)
        send_queries(beside, beside_class)

    gains = (
        video_query_gain_in,
        video_key_gain_in,
        audio_query_gain_in,
        audio_key_gain_in,
    )
    for index, gain in enumerate(gains):
        pltpu.make_async_copy(gain, all_gains.at[pl.ds(index * n, n), :], gain_sem).start()
    for kind in range(len(ins)):
        own_in(kind).start()

    ones = jnp.ones((arows * n, HEAD_DIM), jnp.bfloat16)
    av[:, HEAD_DIM:] = ones
    audio_self[:, HEAD_DIM:] = ones
    ones = jnp.ones((rows * n, HEAD_DIM), jnp.bfloat16)
    vv[:, HEAD_DIM:] = ones
    audio_sum[...] = jnp.zeros_like(audio_sum)

    others = mates + beside + far_middle + far_edge

    def dot_t(left, right):
        return lax.dot_general(
            left, right, (((1,), (1,)), ((), ())), preferred_element_type=jnp.float32
        )

    def dot(left, right):
        return jnp.dot(left, right, preferred_element_type=jnp.float32)

    def self_attend(queries, key_rows, values):
        scores = dot_t(queries, key_rows)
        largest = jnp.max(scores, axis=1, keepdims=True)
        weights = jnp.exp2((scores - largest) * EXP2_SCALE).astype(jnp.bfloat16)
        both = dot(weights, values)
        return (both[:, :HEAD_DIM] / both[:, HEAD_DIM:]).astype(jnp.bfloat16)

    def unit(tokens):
        entries = tokens.astype(jnp.float32)
        mean = jnp.mean(entries * entries, axis=1, keepdims=True)
        return entries * lax.rsqrt(mean + 1e-06)

    def own_gain(index):
        return all_gains[pl.ds(index * n + me, 1), :]

    wait_bytes(all_gains, gain_sem)
    for kind in early:
        wait_in(kind)
    tokens = self_attend(aq[...], ak[...], av[...])
    audio_self[:, :HEAD_DIM] = tokens
    scaled = unit(tokens)
    audio_queries[...] = (scaled * own_gain(2)).astype(jnp.bfloat16)
    audio_keys[...] = (scaled * own_gain(3)).astype(jnp.bfloat16)

    for kind in keys:
        wait_in(kind)

    @pl.when(edge)
    def _():
        send_queries(far_edge + far_middle, far_class)


    def self_part(peers):
        here = [token_rows(peer, rows) for peer in peers]
        tokens = self_attend(jnp.concatenate([vq[one, :] for one in here], 0), vk[...], vv[...])
        scaled = unit(tokens)
        queries = (scaled * own_gain(0)).astype(jnp.bfloat16)
        key_rows = (scaled * own_gain(1)).astype(jnp.bfloat16)
        return tokens, queries, key_rows

    def audio_part(tokens, key_rows):
        weights = jnp.exp2(dot_t(audio_queries[...], key_rows) * EXP2_SCALE)
        values = jnp.concatenate([tokens, jnp.ones_like(tokens)], 1)
        audio_sum[...] += dot(weights.astype(jnp.bfloat16), values)

    def video_part(peers, tokens, queries):
        weights = jnp.exp2(dot_t(queries, audio_keys[...]) * EXP2_SCALE)
        both = dot(weights.astype(jnp.bfloat16), audio_self[...])
        cross = both[:, :HEAD_DIM] / both[:, HEAD_DIM:]
        mixed = (tokens.astype(jnp.float32) + cross).astype(jnp.bfloat16)
        for index, peer in enumerate(peers):
            video_mixed[token_rows(peer, rows), :] = mixed[index * rows : (index + 1) * rows]

    turns = (0, 1, 3, 2)
    for turn in turns:
        last = turn == turns[-1]
        peers = classes[turn]
        wait_queries(turn)
        tokens, queries, key_rows = self_part(peers)
        if last:
            audio_part(tokens, key_rows)
            both = audio_sum[...]
            cross = both[:, :HEAD_DIM] / both[:, HEAD_DIM:]
            audio_mixed[...] = (
                audio_self[:, :HEAD_DIM].astype(jnp.float32) + cross
            ).astype(jnp.bfloat16)
            own_out(0).start()
            for peer in reversed(others):
                sent_out(0, peer).start()
        video_part(peers, tokens, queries)
        if turn == own_class:
            own_out(1).start()
            peers = peers[1:]
        for peer in peers:
            sent_out(1, peer).start()
        if not last:
            audio_part(tokens, key_rows)

    for kind in range(len(ins)):
        wait_sent_in(kind)
    for kind in range(len(outs)):
        wait_out(kind)


def pass_on_kernel(video_in, audio_in, video_out, audio_out, sem):
    copies = (
        pltpu.make_async_copy(video_in, video_out, sem.at[0]),
        pltpu.make_async_copy(audio_in, audio_out, sem.at[1]),
    )
    for copy in copies:
        copy.start()
    for copy in copies:
        copy.wait()


KERNEL_BYTES = 24 * 2**20


def head_per_device(n, *arrays):
    video_q, audio_q = arrays[0], arrays[3]
    tokens, atokens = video_q.shape[0] * n, audio_q.shape[0] * n
    bf16, f32 = jnp.bfloat16, jnp.float32
    gains = [gain.reshape(n, HEAD_DIM) for gain in arrays[6:]]
    anywhere = pl.BlockSpec(memory_space=pl.ANY)
    operands = [
        pltpu.with_memory_space_constraint(one, pltpu.HBM) for one in (*arrays[:6], *gains)
    ]
    results = pl.pallas_call(
        functools.partial(attend_kernel, n),
        out_shape=(
            jax.ShapeDtypeStruct(video_q.shape, bf16),
            jax.ShapeDtypeStruct(audio_q.shape, bf16),
        ),
        in_specs=[anywhere] * 10,
        out_specs=(anywhere, anywhere),
        scratch_shapes=[
            pltpu.VMEM((tokens, HEAD_DIM), bf16),
            pltpu.VMEM((tokens, HEAD_DIM), bf16),
            pltpu.VMEM((tokens, 2 * HEAD_DIM), bf16),
            pltpu.VMEM((atokens, HEAD_DIM), bf16),
            pltpu.VMEM((atokens, HEAD_DIM), bf16),
            pltpu.VMEM((atokens, 2 * HEAD_DIM), bf16),
            pltpu.VMEM((atokens, 2 * HEAD_DIM), bf16),
            pltpu.VMEM((atokens, HEAD_DIM), bf16),
            pltpu.VMEM((atokens, HEAD_DIM), bf16),
            pltpu.VMEM((atokens, 2 * HEAD_DIM), f32),
            pltpu.VMEM((tokens, HEAD_DIM), bf16),
            pltpu.VMEM((atokens, HEAD_DIM), bf16),
            pltpu.SemaphoreType.DMA((6,)),
            pltpu.SemaphoreType.DMA((5,)),
            pltpu.SemaphoreType.DMA((4,)),
            pltpu.SemaphoreType.DMA((2,)),
            pltpu.SemaphoreType.DMA((2,)),
            pltpu.SemaphoreType.REGULAR((7,)),
            pltpu.VMEM((4 * n, HEAD_DIM), f32),
            pltpu.SemaphoreType.DMA,
        ],
        compiler_params=pltpu.CompilerParams(
            collective_id=0, has_side_effects=True, vmem_limit_bytes=KERNEL_BYTES
        ),
    )(*operands)
    return pl.pallas_call(
        pass_on_kernel,
        out_shape=(
            jax.ShapeDtypeStruct(video_q.shape, bf16),
            jax.ShapeDtypeStruct(audio_q.shape, bf16),
        ),
        in_specs=[anywhere] * 2,
        out_specs=(anywhere, anywhere),
        scratch_shapes=[pltpu.SemaphoreType.DMA((2,))],
        compiler_params=pltpu.CompilerParams(vmem_limit_bytes=KERNEL_BYTES // 4),
    )(*results)


def solution(mesh):
    in_specs = (
        P(("clips", "seq"), "head"),
        P(("clips", "seq"), "head"),
        P(("clips", "seq"), "head"),
        P(("clips", "seq"), "head"),
        P(("clips", "seq"), "head"),
        P(("clips", "seq"), "head"),
        P("head"),
        P("head"),
        P("head"),
        P("head"),
    )
    out_specs = (P(("clips", "seq"), "head"), P(("clips", "seq"), "head"))
    sizes = dict(mesh.shape)

    def body(*arrays):
        video_q, audio_q = arrays[0], arrays[3]
        if (
            video_q.shape[1] == sizes["seq"] * HEAD_DIM
            and sizes["seq"] == 8
            and video_q.shape[0] % 16 == 0
            and audio_q.shape[0] % 16 == 0
        ):
            return head_per_device(sizes["seq"], *arrays)
        return per_device(*arrays)

    return jax.shard_map(
        body, mesh=mesh, in_specs=in_specs, out_specs=out_specs, check_vma=False
    )
```

```python
import functools
import math

import jax
import jax.numpy as jnp
from jax import lax
from jax.experimental import pallas as pl
from jax.experimental.pallas import tpu as pltpu
from jax.sharding import PartitionSpec as P

HEAD_DIM = 128
EXP2_SCALE = HEAD_DIM ** (-0.5) * math.log2(math.e)


def normed(tokens, gain_row):
    count = tokens.shape[0]
    head_count = tokens.shape[1] // HEAD_DIM
    entries = tokens.astype(jnp.float32).reshape(count, head_count, HEAD_DIM)
    scaled = entries * lax.rsqrt(jnp.mean(entries * entries, axis=2, keepdims=True) + 1e-06)
    return (scaled.reshape(count, head_count * HEAD_DIM) * gain_row).astype(jnp.bfloat16)


def start_state(row_count, head_count):
    return (
        jnp.full((head_count, row_count), -1e30, jnp.float32),
        jnp.zeros((head_count, row_count), jnp.float32),
        jnp.zeros((row_count, head_count, HEAD_DIM), jnp.float32),
    )


def folding(queries, prepare):
    head_count = queries.shape[1]

    def fold_step(state_now, pieces, offset):
        key_rows, values = prepare(pieces)
        key_rows = key_rows.reshape(key_rows.shape[0], head_count, HEAD_DIM)
        values = values.reshape(values.shape[0], head_count, HEAD_DIM)
        scores = jnp.einsum(
            "qhd,khd->hqk", queries, key_rows, preferred_element_type=jnp.float32
        ) * HEAD_DIM ** (-0.5)
        running_max, row_total, accumulated = state_now
        new_max = jnp.maximum(running_max, jnp.max(scores, axis=2))
        rescale = jnp.exp(running_max - new_max)
        weights = jnp.exp(scores - new_max[:, :, None])
        row_total = jnp.sum(weights, axis=2)
        update = jnp.einsum(
            "hqk,khd->qhd", weights.astype(jnp.bfloat16), values, preferred_element_type=jnp.float32
        )
        accumulated = accumulated * rescale.T[:, :, None] + update
        return (new_max, row_total, accumulated)

    return fold_step


def finish(state_now):
    running_max, row_total, accumulated = state_now
    result = accumulated / row_total.T[:, :, None]
    return result.reshape(result.shape[0], result.shape[1] * HEAD_DIM)


def as_heads(tokens):
    return tokens.reshape(tokens.shape[0], tokens.shape[1] // HEAD_DIM, HEAD_DIM)


def keep_pair(pieces):
    return pieces


def per_device(
    video_q,
    video_k,
    video_v,
    audio_q,
    audio_k,
    audio_v,
    video_query_gain,
    video_key_gain,
    audio_query_gain,
    audio_key_gain,
):
    head_count = video_q.shape[1] // HEAD_DIM
    video_rows = video_q.shape[0]
    audio_rows = audio_q.shape[0]
    video_state = folding(as_heads(video_q), keep_pair)(
        start_state(video_rows, head_count),
        (
            lax.all_gather(video_k, "seq", axis=0, tiled=True),
            lax.all_gather(video_v, "seq", axis=0, tiled=True),
        ),
        jnp.int32(0),
    )
    video_self = finish(video_state).astype(jnp.bfloat16)
    audio_state = folding(as_heads(audio_q), keep_pair)(
        start_state(audio_rows, head_count),
        (
            lax.all_gather(audio_k, "seq", axis=0, tiled=True),
            lax.all_gather(audio_v, "seq", axis=0, tiled=True),
        ),
        jnp.int32(0),
    )
    audio_self = finish(audio_state).astype(jnp.bfloat16)
    audio_whole = lax.all_gather(audio_self, "seq", axis=0, tiled=True)
    video_queries = as_heads(normed(video_self, video_query_gain))
    cross_step = folding(video_queries, keep_pair)
    video_cross = finish(
        cross_step(
            start_state(video_rows, head_count),
            (normed(audio_whole, audio_key_gain), audio_whole),
            0,
        )
    )
    audio_queries = normed(audio_self, audio_query_gain)

    def prepare_video(shard_rows):
        return (normed(shard_rows, video_key_gain), shard_rows)

    audio_state_cross = folding(as_heads(audio_queries), prepare_video)(
        start_state(audio_rows, head_count),
        lax.all_gather(video_self, "seq", axis=0, tiled=True),
        jnp.int32(0),
    )
    audio_cross = finish(audio_state_cross)
    video_mixed = (video_self.astype(jnp.float32) + video_cross).astype(jnp.bfloat16)
    audio_mixed = (audio_self.astype(jnp.float32) + audio_cross).astype(jnp.bfloat16)
    return (video_mixed, audio_mixed)


def attend_kernel(
    n,
    video_q,
    video_k,
    video_v,
    audio_q,
    audio_k,
    audio_v,
    video_query_gain_in,
    video_key_gain_in,
    audio_query_gain_in,
    audio_key_gain_in,
    video_out,
    audio_out,
    vq,
    vk,
    vv,
    aq,
    ak,
    av,
    audio_self,
    audio_queries,
    audio_keys,
    audio_sum,
    video_mixed,
    audio_mixed,
    send_sem,
    recv_sem,
    query_sem,
    out_send_sem,
    out_recv_sem,
    in_sem,
    all_gains,
    gain_sem,
):
    me = lax.axis_index("seq")
    rows = video_q.shape[0]
    arows = audio_q.shape[0]

    width = n // 4
    place, lane = me // width, lax.rem(me, width)
    middle = jnp.logical_or(place == 1, place == 2)
    edge = jnp.logical_not(middle)
    inner = lax.select(place < 2, 1, 2)
    outer = lax.select(place < 2, 0, 3)

    def device(column, step):
        return column * width + lax.rem(lane + step, width)

    mates = [device(place, step) for step in range(1, width)]
    beside = [device(inner + outer - place, step) for step in range(width)]
    far_middle = [device(3 - inner, step) for step in range(width)]
    far_edge = [device(3 - outer, step) for step in range(width)]

    def head_columns(index):
        return pl.ds(pl.multiple_of(index * HEAD_DIM, HEAD_DIM), HEAD_DIM)

    def token_rows(index, count):
        return pl.ds(pl.multiple_of(index * count, count), count)

    ins = (
        (audio_k, ak, arows),
        (audio_v, av, arows),
        (audio_q, aq, arows),
        (video_k, vk, rows),
        (video_v, vv, rows),
        (video_q, vq, rows),
    )

    own_class, beside_class, edge_class = 0, 1, 3
    far_class = lax.select(middle, 2, 3)
    middle_line = [(3 - inner) * width + index for index in range(width)]
    edge_line = [(3 - outer) * width + index for index in range(width)]
    classes = ([me] + mates, beside, middle_line, edge_line)

    def landing(kind, turn):
        return query_sem.at[turn] if kind == 5 else recv_sem.at[kind]

    def own_in(kind):
        source, target, count = ins[kind]
        return pltpu.make_async_copy(
            source.at[:, head_columns(me)],
            target.at[token_rows(me, count), pl.ds(0, HEAD_DIM)],
            landing(kind, own_class),
        )

    def sent_in(kind, peer, turn):
        source, target, count = ins[kind]
        return pltpu.make_async_remote_copy(
            src_ref=source.at[:, head_columns(peer)],
            dst_ref=target.at[token_rows(me, count), pl.ds(0, HEAD_DIM)],
            send_sem=send_sem.at[kind],
            recv_sem=landing(kind, turn),
            device_id={"seq": peer},
            device_id_type=pl.DeviceIdType.MESH,
        )

    def wait_bytes(ref, semaphore):
        pltpu.make_async_copy(ref, ref, semaphore).wait()

    def wait_in(kind):
        wait_bytes(ins[kind][1].at[:, pl.ds(0, HEAD_DIM)], recv_sem.at[kind])

    def wait_queries(turn):
        wait_bytes(vq.at[pl.ds(0, width * rows), :], query_sem.at[turn])

    def wait_sent_in(kind):
        source, target, count = ins[kind]
        sent = target.at[pl.ds(0, (n - 1) * count), pl.ds(0, HEAD_DIM)]
        wait_bytes(sent, send_sem.at[kind])

    outs = ((audio_mixed, audio_out, arows), (video_mixed, video_out, rows))

    def own_out(kind):
        source, target, count = outs[kind]
        return pltpu.make_async_copy(
            source.at[token_rows(me, count), :],
            target.at[:, head_columns(me)],
            out_recv_sem.at[kind],
        )

    def sent_out(kind, peer):
        source, target, count = outs[kind]
        return pltpu.make_async_remote_copy(
            src_ref=source.at[token_rows(peer, count), :],
            dst_ref=target.at[:, head_columns(me)],
            send_sem=out_send_sem.at[kind],
            recv_sem=out_recv_sem.at[kind],
            device_id={"seq": peer},
            device_id_type=pl.DeviceIdType.MESH,
        )

    def wait_out(kind):
        source, target, count = outs[kind]
        wait_bytes(source.at[pl.ds(0, (n - 1) * count), :], out_send_sem.at[kind])
        wait_bytes(target, out_recv_sem.at[kind])

    def signal(semaphore, peer):
        pl.semaphore_signal(
            semaphore,
            inc=1,
            device_id={"seq": peer},
            device_id_type=pl.DeviceIdType.MESH,
        )

    def send(kinds, peers):
        for kind in kinds:
            for peer in peers:
                sent_in(kind, peer, None).start()

    def send_queries(peers, turn):
        for peer in peers:
            sent_in(5, peer, turn).start()

    barrier = pltpu.get_barrier_semaphore()
    first_lane = lane == 0
    core = lax.axis_index("head")
    leader = core == 0

    def signal_core(semaphore):
        pl.semaphore_signal(
            semaphore,
            inc=1,
            device_id={"head": 1 - core},
            device_id_type=pl.DeviceIdType.MESH,
        )

    def follow():
        @pl.when(leader)
        def _():
            signal_core(in_sem.at[6])

        @pl.when(jnp.logical_not(leader))
        def _():
            pl.semaphore_wait(in_sem.at[6], 1)

    early, keys = (0, 1, 2), (3, 4)

    @pl.when(middle)
    def _():
        signal(barrier, far_middle[0])
        signal(barrier, beside[0])

        @pl.when(jnp.logical_not(leader))
        def _():
            signal_core(barrier)

        pl.semaphore_wait(barrier, lax.select(first_lane, 1, 2) + lax.select(leader, 1, 0))

        @pl.when(first_lane)
        def _():
            for peer in mates:
                signal(barrier, peer)

        send(early, far_middle[:1])
        send(keys, far_middle[:1])

        @pl.when(first_lane)
        def _():
            pl.semaphore_wait(in_sem.at[0], len(mates))

        @pl.when(jnp.logical_not(first_lane))
        def _():
            signal(in_sem.at[0], me - lane)

        send(early, far_middle[1:])
        pl.semaphore_wait(in_sem.at[1], 1)
        signal(in_sem.at[2], far_middle[0])
        signal(in_sem.at[5], beside[0])
        send(early, beside[:1] + mates)
        pl.semaphore_wait(in_sem.at[2], 1)
        for peer in mates:
            signal(in_sem.at[3], peer)
        send(early, far_edge[:1])
        send(keys, far_edge[:1])
        send(keys, beside[:1] + mates)
        pl.semaphore_wait(in_sem.at[3], len(mates))
        follow()
        signal(in_sem.at[4], beside[0])
        send(early, far_edge[1:] + beside[1:])
        send(keys, far_edge[1:] + beside[1:])
        send(keys, far_middle[1:])
        send_queries(beside, beside_class)
        send_queries(mates, own_class)
        send_queries(far_edge + far_middle, far_class)

    @pl.when(edge)
    def _():
        @pl.when(jnp.logical_not(leader))
        def _():
            signal_core(barrier)

        pl.semaphore_wait(barrier, lax.select(leader, 2, 1))
        signal(in_sem.at[1], beside[0])
        pl.semaphore_wait(in_sem.at[5], 1)
        send(early, far_middle[:1] + beside[:1])
        send(keys, far_middle[:1] + beside[:1])
        pl.semaphore_wait(in_sem.at[4], 1)
        follow()

        send(early, far_edge + far_middle[1:])
        send(keys, far_edge + far_middle[1:])
        send(early, mates + beside[1:])
        send(keys, mates + beside[1:])
        send_queries(mates, own_class)
        send_queries(beside, beside_class)

    gains = (
        video_query_gain_in,
        video_key_gain_in,
        audio_query_gain_in,
        audio_key_gain_in,
    )
    for index, gain in enumerate(gains):
        pltpu.make_async_copy(gain, all_gains.at[pl.ds(index * n, n), :], gain_sem).start()
    for kind in range(len(ins)):
        own_in(kind).start()

    ones = jnp.ones((arows * n, HEAD_DIM), jnp.bfloat16)
    av[:, HEAD_DIM:] = ones
    audio_self[:, HEAD_DIM:] = ones
    ones = jnp.ones((rows * n, HEAD_DIM), jnp.bfloat16)
    vv[:, HEAD_DIM:] = ones
    audio_sum[...] = jnp.zeros_like(audio_sum)

    others = mates + beside + far_middle + far_edge

    def dot_t(left, right):
        return lax.dot_general(
            left, right, (((1,), (1,)), ((), ())), preferred_element_type=jnp.float32
        )

    def dot(left, right):
        return jnp.dot(left, right, preferred_element_type=jnp.float32)

    def self_attend(queries, key_rows, values):
        scores = dot_t(queries, key_rows)
        largest = jnp.max(scores, axis=1, keepdims=True)
        weights = jnp.exp2((scores - largest) * EXP2_SCALE).astype(jnp.bfloat16)
        both = dot(weights, values)
        return (both[:, :HEAD_DIM] / both[:, HEAD_DIM:]).astype(jnp.bfloat16)

    def unit(tokens):
        entries = tokens.astype(jnp.float32)
        mean = jnp.mean(entries * entries, axis=1, keepdims=True)
        return entries * lax.rsqrt(mean + 1e-06)

    def own_gain(index):
        return all_gains[pl.ds(index * n + me, 1), :]

    wait_bytes(all_gains, gain_sem)
    for kind in early:
        wait_in(kind)
    tokens = self_attend(aq[...], ak[...], av[...])
    audio_self[:, :HEAD_DIM] = tokens
    scaled = unit(tokens)
    audio_queries[...] = (scaled * own_gain(2)).astype(jnp.bfloat16)
    audio_keys[...] = (scaled * own_gain(3)).astype(jnp.bfloat16)

    for kind in keys:
        wait_in(kind)

    @pl.when(edge)
    def _():
        send_queries(far_edge + far_middle, far_class)


    def self_part(peers):
        here = [token_rows(peer, rows) for peer in peers]
        tokens = self_attend(jnp.concatenate([vq[one, :] for one in here], 0), vk[...], vv[...])
        scaled = unit(tokens)
        queries = (scaled * own_gain(0)).astype(jnp.bfloat16)
        key_rows = (scaled * own_gain(1)).astype(jnp.bfloat16)
        return tokens, queries, key_rows

    def audio_part(tokens, key_rows):
        weights = jnp.exp2(dot_t(audio_queries[...], key_rows) * EXP2_SCALE)
        values = jnp.concatenate([tokens, jnp.ones_like(tokens)], 1)
        audio_sum[...] += dot(weights.astype(jnp.bfloat16), values)

    def video_part(peers, tokens, queries):
        weights = jnp.exp2(dot_t(queries, audio_keys[...]) * EXP2_SCALE)
        both = dot(weights.astype(jnp.bfloat16), audio_self[...])
        cross = both[:, :HEAD_DIM] / both[:, HEAD_DIM:]
        mixed = (tokens.astype(jnp.float32) + cross).astype(jnp.bfloat16)
        for index, peer in enumerate(peers):
            video_mixed[token_rows(peer, rows), :] = mixed[index * rows : (index + 1) * rows]

    turns = (0, 1, 3, 2)
    for turn in turns:
        last = turn == turns[-1]
        peers = classes[turn]
        wait_queries(turn)
        tokens, queries, key_rows = self_part(peers)
        if last:
            audio_part(tokens, key_rows)
            both = audio_sum[...]
            cross = both[:, :HEAD_DIM] / both[:, HEAD_DIM:]
            audio_mixed[...] = (
                audio_self[:, :HEAD_DIM].astype(jnp.float32) + cross
            ).astype(jnp.bfloat16)
            own_out(0).start()
            for peer in edge_line + middle_line + beside + mates:
                sent_out(0, peer).start()
            for peer in held:
                sent_out(1, peer).start()
        video_part(peers, tokens, queries)
        if turn == own_class:
            own_out(1).start()
            peers = peers[1:]
        if turn == edge_class:
            peers, held = peers[:1], peers[1:]
        for peer in peers:
            sent_out(1, peer).start()
        if not last:
            audio_part(tokens, key_rows)

    for kind in range(len(ins)):
        wait_sent_in(kind)
    for kind in range(len(outs)):
        wait_out(kind)


def pass_on_kernel(video_in, audio_in, video_out, audio_out, sem):
    copies = (
        pltpu.make_async_copy(video_in, video_out, sem.at[0]),
        pltpu.make_async_copy(audio_in, audio_out, sem.at[1]),
    )
    for copy in copies:
        copy.start()
    for copy in copies:
        copy.wait()


KERNEL_BYTES = 24 * 2**20


def head_per_device(n, *arrays):
    video_q, audio_q = arrays[0], arrays[3]
    tokens, atokens = video_q.shape[0] * n, audio_q.shape[0] * n
    bf16, f32 = jnp.bfloat16, jnp.float32
    gains = [gain.reshape(n, HEAD_DIM) for gain in arrays[6:]]
    anywhere = pl.BlockSpec(memory_space=pl.ANY)
    operands = [
        pltpu.with_memory_space_constraint(one, pltpu.HBM) for one in (*arrays[:6], *gains)
    ]
    results = pl.pallas_call(
        functools.partial(attend_kernel, n),
        out_shape=(
            jax.ShapeDtypeStruct(video_q.shape, bf16),
            jax.ShapeDtypeStruct(audio_q.shape, bf16),
        ),
        in_specs=[anywhere] * 10,
        out_specs=(anywhere, anywhere),
        scratch_shapes=[
            pltpu.VMEM((tokens, HEAD_DIM), bf16),
            pltpu.VMEM((tokens, HEAD_DIM), bf16),
            pltpu.VMEM((tokens, 2 * HEAD_DIM), bf16),
            pltpu.VMEM((atokens, HEAD_DIM), bf16),
            pltpu.VMEM((atokens, HEAD_DIM), bf16),
            pltpu.VMEM((atokens, 2 * HEAD_DIM), bf16),
            pltpu.VMEM((atokens, 2 * HEAD_DIM), bf16),
            pltpu.VMEM((atokens, HEAD_DIM), bf16),
            pltpu.VMEM((atokens, HEAD_DIM), bf16),
            pltpu.VMEM((atokens, 2 * HEAD_DIM), f32),
            pltpu.VMEM((tokens, HEAD_DIM), bf16),
            pltpu.VMEM((atokens, HEAD_DIM), bf16),
            pltpu.SemaphoreType.DMA((6,)),
            pltpu.SemaphoreType.DMA((5,)),
            pltpu.SemaphoreType.DMA((4,)),
            pltpu.SemaphoreType.DMA((2,)),
            pltpu.SemaphoreType.DMA((2,)),
            pltpu.SemaphoreType.REGULAR((7,)),
            pltpu.VMEM((4 * n, HEAD_DIM), f32),
            pltpu.SemaphoreType.DMA,
        ],
        compiler_params=pltpu.CompilerParams(
            collective_id=0, has_side_effects=True, vmem_limit_bytes=KERNEL_BYTES
        ),
    )(*operands)
    return pl.pallas_call(
        pass_on_kernel,
        out_shape=(
            jax.ShapeDtypeStruct(video_q.shape, bf16),
            jax.ShapeDtypeStruct(audio_q.shape, bf16),
        ),
        in_specs=[anywhere] * 2,
        out_specs=(anywhere, anywhere),
        scratch_shapes=[pltpu.SemaphoreType.DMA((2,))],
        compiler_params=pltpu.CompilerParams(vmem_limit_bytes=KERNEL_BYTES // 4),
    )(*results)


def solution(mesh):
    in_specs = (
        P(("clips", "seq"), "head"),
        P(("clips", "seq"), "head"),
        P(("clips", "seq"), "head"),
        P(("clips", "seq"), "head"),
        P(("clips", "seq"), "head"),
        P(("clips", "seq"), "head"),
        P("head"),
        P("head"),
        P("head"),
        P("head"),
    )
    out_specs = (P(("clips", "seq"), "head"), P(("clips", "seq"), "head"))
    sizes = dict(mesh.shape)

    def body(*arrays):
        video_q, audio_q = arrays[0], arrays[3]
        if (
            video_q.shape[1] == sizes["seq"] * HEAD_DIM
            and sizes["seq"] == 8
            and video_q.shape[0] % 16 == 0
            and audio_q.shape[0] % 16 == 0
        ):
            return head_per_device(sizes["seq"], *arrays)
        return per_device(*arrays)

    return jax.shard_map(
        body, mesh=mesh, in_specs=in_specs, out_specs=out_specs, check_vma=False
    )
```

```python
import functools
import math

import jax
import jax.numpy as jnp
from jax import lax
from jax.experimental import pallas as pl
from jax.experimental.pallas import tpu as pltpu
from jax.sharding import PartitionSpec as P

HEAD_DIM = 128
EXP2_SCALE = HEAD_DIM ** (-0.5) * math.log2(math.e)


def normed(tokens, gain_row):
    count = tokens.shape[0]
    head_count = tokens.shape[1] // HEAD_DIM
    entries = tokens.astype(jnp.float32).reshape(count, head_count, HEAD_DIM)
    scaled = entries * lax.rsqrt(jnp.mean(entries * entries, axis=2, keepdims=True) + 1e-06)
    return (scaled.reshape(count, head_count * HEAD_DIM) * gain_row).astype(jnp.bfloat16)


def start_state(row_count, head_count):
    return (
        jnp.full((head_count, row_count), -1e30, jnp.float32),
        jnp.zeros((head_count, row_count), jnp.float32),
        jnp.zeros((row_count, head_count, HEAD_DIM), jnp.float32),
    )


def folding(queries, prepare):
    head_count = queries.shape[1]

    def fold_step(state_now, pieces, offset):
        key_rows, values = prepare(pieces)
        key_rows = key_rows.reshape(key_rows.shape[0], head_count, HEAD_DIM)
        values = values.reshape(values.shape[0], head_count, HEAD_DIM)
        scores = jnp.einsum(
            "qhd,khd->hqk", queries, key_rows, preferred_element_type=jnp.float32
        ) * HEAD_DIM ** (-0.5)
        running_max, row_total, accumulated = state_now
        new_max = jnp.maximum(running_max, jnp.max(scores, axis=2))
        rescale = jnp.exp(running_max - new_max)
        weights = jnp.exp(scores - new_max[:, :, None])
        row_total = jnp.sum(weights, axis=2)
        update = jnp.einsum(
            "hqk,khd->qhd", weights.astype(jnp.bfloat16), values, preferred_element_type=jnp.float32
        )
        accumulated = accumulated * rescale.T[:, :, None] + update
        return (new_max, row_total, accumulated)

    return fold_step


def finish(state_now):
    running_max, row_total, accumulated = state_now
    result = accumulated / row_total.T[:, :, None]
    return result.reshape(result.shape[0], result.shape[1] * HEAD_DIM)


def as_heads(tokens):
    return tokens.reshape(tokens.shape[0], tokens.shape[1] // HEAD_DIM, HEAD_DIM)


def keep_pair(pieces):
    return pieces


def per_device(
    video_q,
    video_k,
    video_v,
    audio_q,
    audio_k,
    audio_v,
    video_query_gain,
    video_key_gain,
    audio_query_gain,
    audio_key_gain,
):
    head_count = video_q.shape[1] // HEAD_DIM
    video_rows = video_q.shape[0]
    audio_rows = audio_q.shape[0]
    video_state = folding(as_heads(video_q), keep_pair)(
        start_state(video_rows, head_count),
        (
            lax.all_gather(video_k, "seq", axis=0, tiled=True),
            lax.all_gather(video_v, "seq", axis=0, tiled=True),
        ),
        jnp.int32(0),
    )
    video_self = finish(video_state).astype(jnp.bfloat16)
    audio_state = folding(as_heads(audio_q), keep_pair)(
        start_state(audio_rows, head_count),
        (
            lax.all_gather(audio_k, "seq", axis=0, tiled=True),
            lax.all_gather(audio_v, "seq", axis=0, tiled=True),
        ),
        jnp.int32(0),
    )
    audio_self = finish(audio_state).astype(jnp.bfloat16)
    audio_whole = lax.all_gather(audio_self, "seq", axis=0, tiled=True)
    video_queries = as_heads(normed(video_self, video_query_gain))
    cross_step = folding(video_queries, keep_pair)
    video_cross = finish(
        cross_step(
            start_state(video_rows, head_count),
            (normed(audio_whole, audio_key_gain), audio_whole),
            0,
        )
    )
    audio_queries = normed(audio_self, audio_query_gain)

    def prepare_video(shard_rows):
        return (normed(shard_rows, video_key_gain), shard_rows)

    audio_state_cross = folding(as_heads(audio_queries), prepare_video)(
        start_state(audio_rows, head_count),
        lax.all_gather(video_self, "seq", axis=0, tiled=True),
        jnp.int32(0),
    )
    audio_cross = finish(audio_state_cross)
    video_mixed = (video_self.astype(jnp.float32) + video_cross).astype(jnp.bfloat16)
    audio_mixed = (audio_self.astype(jnp.float32) + audio_cross).astype(jnp.bfloat16)
    return (video_mixed, audio_mixed)


def attend_kernel(
    n,
    video_q,
    video_k,
    video_v,
    audio_q,
    audio_k,
    audio_v,
    video_query_gain_in,
    video_key_gain_in,
    audio_query_gain_in,
    audio_key_gain_in,
    video_out,
    audio_out,
    vq,
    vk,
    vv,
    aq,
    ak,
    av,
    audio_self,
    audio_queries,
    audio_keys,
    audio_sum,
    video_mixed,
    audio_mixed,
    send_sem,
    recv_sem,
    query_sem,
    out_send_sem,
    out_recv_sem,
    in_sem,
    all_gains,
    gain_sem,
):
    me = lax.axis_index("seq")
    rows = video_q.shape[0]
    arows = audio_q.shape[0]

    width = n // PLACES
    place, lane = me // width, lax.rem(me, width)
    middle = jnp.logical_or(place == 1, place == 2)
    edge = jnp.logical_not(middle)
    inner = lax.select(place < 2, 1, 2)
    outer = lax.select(place < 2, 0, 3)

    def device(column, step):
        return column * width + lax.rem(lane + step, width)

    mates = [device(place, step) for step in range(1, width)]
    beside = [device(inner + outer - place, step) for step in range(width)]
    far_middle = [device(3 - inner, step) for step in range(width)]
    far_edge = [device(3 - outer, step) for step in range(width)]

    def head_columns(index):
        return pl.ds(pl.multiple_of(index * HEAD_DIM, HEAD_DIM), HEAD_DIM)

    def token_rows(index, count):
        return pl.ds(pl.multiple_of(index * count, count), count)

    ins = (
        (audio_k, ak, arows),
        (audio_v, av, arows),
        (audio_q, aq, arows),
        (video_k, vk, rows),
        (video_v, vv, rows),
        (video_q, vq, rows),
    )

    own_class, beside_class, edge_class = 0, 1, 3
    far_class = lax.select(middle, 2, 3)
    middle_line = [(3 - inner) * width + index for index in range(width)]
    edge_line = [(3 - outer) * width + index for index in range(width)]
    classes = ([me] + mates, beside, middle_line, edge_line)

    def landing(kind, turn):
        return query_sem.at[turn] if kind == 5 else recv_sem.at[kind]

    def own_in(kind):
        source, target, count = ins[kind]
        return pltpu.make_async_copy(
            source.at[:, head_columns(me)],
            target.at[token_rows(me, count), pl.ds(0, HEAD_DIM)],
            landing(kind, own_class),
        )

    def sent_in(kind, peer, turn):
        source, target, count = ins[kind]
        return pltpu.make_async_remote_copy(
            src_ref=source.at[:, head_columns(peer)],
            dst_ref=target.at[token_rows(me, count), pl.ds(0, HEAD_DIM)],
            send_sem=send_sem.at[kind],
            recv_sem=landing(kind, turn),
            device_id={"seq": peer},
            device_id_type=pl.DeviceIdType.MESH,
        )

    def wait_bytes(ref, semaphore):
        pltpu.make_async_copy(ref, ref, semaphore).wait()

    def wait_in(kind):
        wait_bytes(ins[kind][1].at[:, pl.ds(0, HEAD_DIM)], recv_sem.at[kind])

    def wait_queries(turn):
        wait_bytes(vq.at[pl.ds(0, width * rows), :], query_sem.at[turn])

    def wait_sent_in(kind):
        source, target, count = ins[kind]
        sent = target.at[pl.ds(0, (n - 1) * count), pl.ds(0, HEAD_DIM)]
        wait_bytes(sent, send_sem.at[kind])

    outs = ((audio_mixed, audio_out, arows), (video_mixed, video_out, rows))

    def own_out(kind):
        source, target, count = outs[kind]
        return pltpu.make_async_copy(
            source.at[token_rows(me, count), :],
            target.at[:, head_columns(me)],
            out_recv_sem.at[kind],
        )

    def sent_out(kind, peer):
        source, target, count = outs[kind]
        return pltpu.make_async_remote_copy(
            src_ref=source.at[token_rows(peer, count), :],
            dst_ref=target.at[:, head_columns(me)],
            send_sem=out_send_sem.at[kind],
            recv_sem=out_recv_sem.at[kind],
            device_id={"seq": peer},
            device_id_type=pl.DeviceIdType.MESH,
        )

    def wait_out(kind):
        source, target, count = outs[kind]
        wait_bytes(source.at[pl.ds(0, (n - 1) * count), :], out_send_sem.at[kind])
        wait_bytes(target, out_recv_sem.at[kind])

    def signal(semaphore, peer):
        pl.semaphore_signal(
            semaphore,
            inc=1,
            device_id={"seq": peer},
            device_id_type=pl.DeviceIdType.MESH,
        )

    def send(kinds, peers):
        for kind in kinds:
            for peer in peers:
                sent_in(kind, peer, None).start()

    def send_queries(peers, turn):
        for peer in peers:
            sent_in(5, peer, turn).start()

    barrier = pltpu.get_barrier_semaphore()
    first_lane = lane == 0
    core = lax.axis_index("head")
    leader = core == 0

    def signal_core(semaphore):
        pl.semaphore_signal(
            semaphore,
            inc=1,
            device_id={"head": 1 - core},
            device_id_type=pl.DeviceIdType.MESH,
        )

    def follow():
        @pl.when(leader)
        def _():
            signal_core(in_sem.at[6])

        @pl.when(jnp.logical_not(leader))
        def _():
            pl.semaphore_wait(in_sem.at[6], 1)

    early, keys = (0, 1, 2), (3, 4)

    @pl.when(middle)
    def _():
        signal(barrier, far_middle[0])
        signal(barrier, beside[0])

        @pl.when(first_lane)
        def _():
            for peer in mates:
                signal(barrier, peer)


        @pl.when(jnp.logical_not(leader))
        def _():
            signal_core(barrier)

        pl.semaphore_wait(barrier, lax.select(first_lane, 1, 2) + lax.select(leader, 1, 0))

        @pl.when(jnp.logical_not(first_lane))
        def _():
            signal(in_sem.at[7], far_middle[0])
            signal(in_sem.at[0], me - lane)

        send(early, far_middle[:1])
        send(keys, far_middle[:1])

        pl.semaphore_wait(in_sem.at[1], 1)
        signal(in_sem.at[2], far_middle[0])
        signal(in_sem.at[5], beside[0])
        @pl.when(first_lane)
        def _():
            pl.semaphore_wait(in_sem.at[0], len(mates))

        @pl.when(jnp.logical_not(first_lane))
        def _():
            pl.semaphore_wait(in_sem.at[7], 1)

        send(early, far_middle[1:])
        send(early, beside[:1] + mates)
        pl.semaphore_wait(in_sem.at[2], 1)
        for peer in mates:
            signal(in_sem.at[3], peer)
        send(early, far_edge[:1])
        send(keys, far_edge[:1])
        send(keys, beside[:1] + mates)
        pl.semaphore_wait(in_sem.at[3], len(mates))
        follow()
        signal(in_sem.at[4], beside[0])
        send(early, far_edge[1:] + beside[1:])
        send(keys, far_edge[1:] + beside[1:])
        send(keys, far_middle[1:])
        send_queries(beside, beside_class)
        send_queries(mates, own_class)
        send_queries(far_edge + far_middle, far_class)

    @pl.when(edge)
    def _():
        @pl.when(jnp.logical_not(leader))
        def _():
            signal_core(barrier)

        pl.semaphore_wait(barrier, lax.select(leader, 2, 1))
        signal(in_sem.at[1], beside[0])
        pl.semaphore_wait(in_sem.at[5], 1)
        send(early, far_middle[:1] + beside[:1])
        send(keys, far_middle[:1] + beside[:1])
        pl.semaphore_wait(in_sem.at[4], 1)
        follow()

        send(early, far_edge + far_middle[1:])
        send(keys, far_edge + far_middle[1:])
        send(early, mates + beside[1:])
        send(keys, mates + beside[1:])
        send_queries(mates, own_class)
        send_queries(beside, beside_class)

    gains = (
        video_query_gain_in,
        video_key_gain_in,
        audio_query_gain_in,
        audio_key_gain_in,
    )
    for index, gain in enumerate(gains):
        pltpu.make_async_copy(gain, all_gains.at[pl.ds(index * n, n), :], gain_sem).start()
    for kind in range(len(ins)):
        own_in(kind).start()

    ones = jnp.ones((arows * n, HEAD_DIM), jnp.bfloat16)
    av[:, HEAD_DIM:] = ones
    audio_self[:, HEAD_DIM:] = ones
    ones = jnp.ones((rows * n, HEAD_DIM), jnp.bfloat16)
    vv[:, HEAD_DIM:] = ones
    audio_sum[...] = jnp.zeros_like(audio_sum)

    others = mates + beside + far_middle + far_edge

    def dot_t(left, right):
        return lax.dot_general(
            left, right, (((1,), (1,)), ((), ())), preferred_element_type=jnp.float32
        )

    def dot(left, right):
        return jnp.dot(left, right, preferred_element_type=jnp.float32)

    def self_attend(queries, key_rows, values):
        scores = dot_t(queries, key_rows)
        largest = jnp.max(scores, axis=1, keepdims=True)
        weights = jnp.exp2((scores - largest) * EXP2_SCALE).astype(jnp.bfloat16)
        both = dot(weights, values)
        return (both[:, :HEAD_DIM] / both[:, HEAD_DIM:]).astype(jnp.bfloat16)

    def unit(tokens):
        entries = tokens.astype(jnp.float32)
        mean = jnp.mean(entries * entries, axis=1, keepdims=True)
        return entries * lax.rsqrt(mean + 1e-06)

    def own_gain(index):
        return all_gains[pl.ds(index * n + me, 1), :]

    wait_bytes(all_gains, gain_sem)
    for kind in early:
        wait_in(kind)
    tokens = self_attend(aq[...], ak[...], av[...])
    audio_self[:, :HEAD_DIM] = tokens
    scaled = unit(tokens)
    audio_queries[...] = (scaled * own_gain(2)).astype(jnp.bfloat16)
    audio_keys[...] = (scaled * own_gain(3)).astype(jnp.bfloat16)

    for kind in keys:
        wait_in(kind)

    @pl.when(edge)
    def _():
        send_queries(far_edge + far_middle, far_class)


    def self_part(peers):
        here = [token_rows(peer, rows) for peer in peers]
        tokens = self_attend(jnp.concatenate([vq[one, :] for one in here], 0), vk[...], vv[...])
        scaled = unit(tokens)
        queries = (scaled * own_gain(0)).astype(jnp.bfloat16)
        key_rows = (scaled * own_gain(1)).astype(jnp.bfloat16)
        return tokens, queries, key_rows

    def audio_part(tokens, key_rows):
        weights = jnp.exp2(dot_t(audio_queries[...], key_rows) * EXP2_SCALE)
        values = jnp.concatenate([tokens, jnp.ones_like(tokens)], 1)
        audio_sum[...] += dot(weights.astype(jnp.bfloat16), values)

    def video_part(peers, tokens, queries):
        weights = jnp.exp2(dot_t(queries, audio_keys[...]) * EXP2_SCALE)
        both = dot(weights.astype(jnp.bfloat16), audio_self[...])
        cross = both[:, :HEAD_DIM] / both[:, HEAD_DIM:]
        mixed = (tokens.astype(jnp.float32) + cross).astype(jnp.bfloat16)
        for index, peer in enumerate(peers):
            video_mixed[token_rows(peer, rows), :] = mixed[index * rows : (index + 1) * rows]

    turns = (0, 1, 3, 2)
    for turn in turns:
        last = turn == turns[-1]
        peers = classes[turn]
        wait_queries(turn)
        tokens, queries, key_rows = self_part(peers)
        if last:
            audio_part(tokens, key_rows)
            both = audio_sum[...]
            cross = both[:, :HEAD_DIM] / both[:, HEAD_DIM:]
            audio_mixed[...] = (
                audio_self[:, :HEAD_DIM].astype(jnp.float32) + cross
            ).astype(jnp.bfloat16)
            own_out(0).start()
            for peer in edge_line:
                sent_out(0, peer).start()
            for peer in held:
                sent_out(1, peer).start()
            for peer in middle_line:
                sent_out(0, peer).start()
        video_part(peers, tokens, queries)
        if turn == own_class:
            own_out(1).start()
            peers = peers[1:]
        if turn == edge_class:
            peers, held = peers[:1], peers[1:]
        for peer in peers:
            sent_out(1, peer).start()
        if last:
            for peer in beside + mates:
                sent_out(0, peer).start()
        if not last:
            audio_part(tokens, key_rows)

    for kind in range(len(ins)):
        wait_sent_in(kind)
    for kind in range(len(outs)):
        wait_out(kind)


def pass_on_kernel(video_in, audio_in, video_out, audio_out, sem):
    copies = (
        pltpu.make_async_copy(video_in, video_out, sem.at[0]),
        pltpu.make_async_copy(audio_in, audio_out, sem.at[1]),
    )
    for copy in copies:
        copy.start()
    for copy in copies:
        copy.wait()


PLACES, LANES = 4, 2
KERNEL_BYTES = 24 * 2**20


def head_per_device(n, *arrays):
    video_q, audio_q = arrays[0], arrays[3]
    tokens, atokens = video_q.shape[0] * n, audio_q.shape[0] * n
    bf16, f32 = jnp.bfloat16, jnp.float32
    gains = [gain.reshape(n, HEAD_DIM) for gain in arrays[6:]]
    anywhere = pl.BlockSpec(memory_space=pl.ANY)
    operands = [
        pltpu.with_memory_space_constraint(one, pltpu.HBM) for one in (*arrays[:6], *gains)
    ]
    results = pl.pallas_call(
        functools.partial(attend_kernel, n),
        out_shape=(
            jax.ShapeDtypeStruct(video_q.shape, bf16),
            jax.ShapeDtypeStruct(audio_q.shape, bf16),
        ),
        in_specs=[anywhere] * 10,
        out_specs=(anywhere, anywhere),
        scratch_shapes=[
            pltpu.VMEM((tokens, HEAD_DIM), bf16),
            pltpu.VMEM((tokens, HEAD_DIM), bf16),
            pltpu.VMEM((tokens, 2 * HEAD_DIM), bf16),
            pltpu.VMEM((atokens, HEAD_DIM), bf16),
            pltpu.VMEM((atokens, HEAD_DIM), bf16),
            pltpu.VMEM((atokens, 2 * HEAD_DIM), bf16),
            pltpu.VMEM((atokens, 2 * HEAD_DIM), bf16),
            pltpu.VMEM((atokens, HEAD_DIM), bf16),
            pltpu.VMEM((atokens, HEAD_DIM), bf16),
            pltpu.VMEM((atokens, 2 * HEAD_DIM), f32),
            pltpu.VMEM((tokens, HEAD_DIM), bf16),
            pltpu.VMEM((atokens, HEAD_DIM), bf16),
            pltpu.SemaphoreType.DMA((6,)),
            pltpu.SemaphoreType.DMA((5,)),
            pltpu.SemaphoreType.DMA((4,)),
            pltpu.SemaphoreType.DMA((2,)),
            pltpu.SemaphoreType.DMA((2,)),
            pltpu.SemaphoreType.REGULAR((8,)),
            pltpu.VMEM((4 * n, HEAD_DIM), f32),
            pltpu.SemaphoreType.DMA,
        ],
        compiler_params=pltpu.CompilerParams(
            collective_id=0, has_side_effects=True, vmem_limit_bytes=KERNEL_BYTES
        ),
    )(*operands)
    return pl.pallas_call(
        pass_on_kernel,
        out_shape=(
            jax.ShapeDtypeStruct(video_q.shape, bf16),
            jax.ShapeDtypeStruct(audio_q.shape, bf16),
        ),
        in_specs=[anywhere] * 2,
        out_specs=(anywhere, anywhere),
        scratch_shapes=[pltpu.SemaphoreType.DMA((2,))],
        compiler_params=pltpu.CompilerParams(vmem_limit_bytes=KERNEL_BYTES // 4),
    )(*results)


def solution(mesh):
    in_specs = (
        P(("clips", "seq"), "head"),
        P(("clips", "seq"), "head"),
        P(("clips", "seq"), "head"),
        P(("clips", "seq"), "head"),
        P(("clips", "seq"), "head"),
        P(("clips", "seq"), "head"),
        P("head"),
        P("head"),
        P("head"),
        P("head"),
    )
    out_specs = (P(("clips", "seq"), "head"), P(("clips", "seq"), "head"))
    sizes = dict(mesh.shape)

    def body(*arrays):
        video_q, audio_q = arrays[0], arrays[3]
        if (
            video_q.shape[1] == sizes["seq"] * HEAD_DIM
            and sizes["seq"] == PLACES * LANES
            and sizes["head"] == 2
            and video_q.shape[0] % 16 == 0
            and audio_q.shape[0] % 16 == 0
        ):
            return head_per_device(sizes["seq"], *arrays)
        return per_device(*arrays)

    return jax.shard_map(
        body, mesh=mesh, in_specs=in_specs, out_specs=out_specs, check_vma=False
    )
```
